32 devices in a mesh: section: 4 (over z), dp: 8 (over y, x, core).
Axes of the slice: x: 2, y: 2, z: 4, core: 2. Of those that a mesh axis runs over, the one named last changes fastest.
Arguments:
- embedded: bfloat16 [2, 1024, 4096], P(None, 'dp'), may hold values from -6 to 6
- saved_inputs: bfloat16 [4, 2, 1024, 4096], P('section', None, 'dp'), may hold values from -6 to 6
- cotangent: bfloat16 [2, 1024, 4096], P(None, 'dp'), may hold values from -6 to 6
- w_down: bfloat16 [4, 512, 4096], P('section'), may hold values from -0.09375 to 0.09375
- w_up: bfloat16 [4, 512, 4096], P('section'), may hold values from -0.046875 to 0.046875
- bias: float32 [4, 4096], P('section'), may hold values from -3 to 3
- owners: int32 [1024, 2, 16, 1], P('dp'), may hold values from 0 to 31; in each aligned block of 1024 rows (0 to 1023, 1024 to 2047, ..., all dimensions but the last counted through in order) at most 64 rows name the same one
- row_ids: int32 [1024, 2, 16], P('dp'), may hold values from 0 to 2047
Outputs:
- grad_down: float32 [4, 512, 4096], P('section', None, 'dp')
- grad_up: float32 [4, 512, 4096], P('section', None, 'dp')
- grad_bias: float32 [4, 4096], P('section', 'dp')
- table_grad: float32 [65536, 256], P(('section', 'dp'))
The draws below stay inside these ranges and needn't reach their ends.
Inputs may be any that keep to these rules, and one draw needn't show every extreme that they name: `owners`: in each aligned block of 1024 lookups in the order (sample, micro-batch, feature) no owner is named more than 64 times, a bound that some block reaches.
All inputs are finite; a program needn't handle non-finite values.
Results may differ from the reference program's by a relative error of at most 0.015.
Values may be sent and summed in bfloat16 or wider, within the bound.
A program may use at most 192 MiB of HBM per device.

```python
import math
import jax
import jax.numpy as jnp
import numpy as np

D = 4096
E = 256
R = 512
MB = 2
ROWS_DEV = 2048
F = 16
LAYERS = 4
BATCH = 1024
LOOK = 1024
CAP = 64
N_SECTION = 4
N_DP = 8


def touch_ends(entries, stream_key, least, largest):
    longest = entries.shape.index(max(entries.shape))
    spots = []
    for shift in (0, 1):
        where = [jax.random.randint(jax.random.fold_in(stream_key, axis), (), 0, length) for axis, length in enumerate(entries.shape)]
        where[longest] = (where[longest] + shift) % entries.shape[longest]
        spots.append(tuple(where))
    return entries.at[spots[0]].set(least).at[spots[1]].set(largest)


def block_levels(key, extent, pieces, smallest, largest):
    gain, own = 1.0, jax.random.fold_in(key, 6)
    for position, parts in pieces:
        draws = jnp.exp(jax.random.uniform(jax.random.fold_in(own, position), (parts,), jnp.float32, smallest / len(pieces), largest / len(pieces)))
        gain = gain * jnp.repeat(draws, extent[position] // parts).reshape([-1 if axis == position else 1 for axis in range(len(extent))])
    return gain


def routed_block(own_key, own, number, rows, amount, top, bound, slope):
    sequence = jax.random.permutation(own_key, amount)
    crowded, usual = shares(amount, rows * top, bound, slope, True), shares(amount, rows * top, bound, slope, False)
    places = jnp.arange(amount)

    def named(lengths, rotation):
        used = int((lengths > 0).sum())
        fixed = max(1, used // 4)
        moved = fixed + (places - fixed + rotation * (used - fixed)) % max(1, amount - fixed)
        return jnp.zeros((amount,), jnp.int32).at[sequence[jnp.where(places < fixed, places, moved)]].set(jnp.asarray(lengths, jnp.int32))

    lengths = jnp.where(number % 4 == 0, named(crowded, number // 4), named(usual, number - number // 4 - 1))
    mixed = jax.random.permutation(jax.random.fold_in(own, 3), amount)
    source_of, taker = mixed[0:amount // 2 * 2:2], mixed[1:amount // 2 * 2:2]
    slack = jnp.minimum(lengths[source_of] - 1, bound - lengths[taker]) // 2
    slack = jnp.where((source_of == sequence[0]) | (taker == sequence[0]) | (lengths[taker] == 0), 0, jnp.maximum(slack, 0))
    moved = jax.random.randint(jax.random.fold_in(own, 4), (amount // 2,), 0, 1 << 20) % (slack + 1)
    lengths = lengths.at[source_of].add(-moved).at[taker].add(moved)
    items = jnp.searchsorted(jnp.cumsum(lengths), jnp.arange(rows * top), side="right").astype(jnp.int32)
    listing = items.reshape(top, rows).T
    listing = listing[jax.random.permutation(jax.random.fold_in(own, 1), rows)]
    rotation = jax.random.randint(jax.random.fold_in(own, 2), (rows, 1), 0, top)
    return jnp.take_along_axis(listing, (jnp.arange(top)[None, :] + rotation) % top, axis=1)


def shares(count, total, limit, slope, full):
    portions = [(1 << 20) // math.isqrt(grade ** slope) + 1 for grade in range(1, count + 1)]
    largest = limit if full else min(limit, max(-(-total // count), total * portions[0] // sum(portions)))
    least = 1 if total - largest >= count - 1 else 0
    counts, spare = [largest] + [least] * (count - 1), total - largest - least * (count - 1)
    while spare > 0:
        free = [i for i in range(1, count) if counts[i] < largest] or [i for i in range(1, count) if counts[i] < limit]
        mass, remaining = sum([portions[i] for i in free]), spare
        for i in free:
            addition = min(limit - counts[i], max(1, remaining * portions[i] // mass), spare)
            counts[i] = counts[i] + addition
            spare = spare - addition
    return np.array(counts)


def normal_values(rng, shape, spread, bound, cuts=(), dtype=jnp.bfloat16):
    array = spread * jax.random.normal(rng, shape, jnp.float32)
    if cuts:
        array = array * block_levels(rng, shape, cuts, -0.22, 0.18)
    return jnp.clip(array, -bound, bound).astype(dtype)


def setup_inputs(seed: int = 0) -> dict:
    splits = jax.random.split(jax.random.key(seed), 9)
    embedded = normal_values(splits[0], (MB, BATCH, D), 1.0, 6.0, ((1, 8),))
    saved_inputs = normal_values(splits[1], (LAYERS, MB, BATCH, D), 1.0, 6.0, ((0, 4), (2, 8)))
    cotangent = normal_values(splits[2], (MB, BATCH, D), 1.0, 6.0, ((1, 8),))
    w_down = normal_values(splits[3], (LAYERS, R, D), D ** -0.5, 0.09375, ((0, 4),))
    w_up = normal_values(splits[4], (LAYERS, R, D), (4 * D) ** -0.5, 0.046875, ((0, 4),))
    bias = normal_values(splits[5], (LAYERS, D), 0.5, 3.0, ((0, 4),), jnp.float32)
    owners_keys = jax.random.split(jax.random.fold_in(splits[6], 1), BATCH * MB * F // LOOK)
    owners_turns = jax.random.permutation(jax.random.fold_in(splits[6], 3), BATCH * MB * F // LOOK)
    owners = jax.vmap(lambda own, number: routed_block(jax.random.fold_in(splits[6], 2), own, number, LOOK, N_SECTION * N_DP, 1, CAP, 2))(owners_keys, owners_turns).reshape((BATCH, MB, F, 1))
    row_ids = touch_ends(jax.random.randint(splits[7], (BATCH, MB, F), 0, ROWS_DEV), jax.random.fold_in(splits[7], 1), 0, ROWS_DEV - 1).astype(jnp.int32)
    return {"embedded": embedded, "saved_inputs": saved_inputs, "cotangent": cotangent, "w_down": w_down, "w_up": w_up, "bias": bias, "owners": owners, "row_ids": row_ids}


def reference(embedded, saved_inputs, cotangent, w_down, w_up, bias, owners, row_ids):
    grad_down = jnp.zeros((LAYERS, R, D), jnp.float32)
    grad_up = jnp.zeros((LAYERS, R, D), jnp.float32)
    grad_bias = jnp.zeros((LAYERS, D), jnp.float32)
    input_grads = []
    for micro in range(MB):
        first = embedded[micro].astype(jnp.float32)
        incoming = cotangent[micro]
        total = jnp.zeros((BATCH, D), jnp.float32)
        for layer in range(LAYERS - 1, -1, -1):
            layer_in = saved_inputs[layer, micro]
            latent = jnp.dot(layer_in, w_down[layer].T, preferred_element_type=jnp.float32).astype(jnp.bfloat16)
            product = jnp.dot(latent, w_up[layer], preferred_element_type=jnp.float32) + bias[layer]
            upstream = incoming.astype(jnp.float32)
            grad_prod = upstream * first
            total = total + upstream * product
            grad_prod_b = grad_prod.astype(jnp.bfloat16)
            grad_up = grad_up.at[layer].add(jnp.dot(latent.T, grad_prod_b, preferred_element_type=jnp.float32))
            grad_bias = grad_bias.at[layer].add(jnp.sum(grad_prod, axis=0))
            grad_latent = jnp.dot(grad_prod_b, w_up[layer].T, preferred_element_type=jnp.float32).astype(jnp.bfloat16)
            grad_down = grad_down.at[layer].add(jnp.dot(grad_latent.T, layer_in, preferred_element_type=jnp.float32))
            passed = upstream + jnp.dot(grad_latent, w_down[layer], preferred_element_type=jnp.float32)
            if layer > 0:
                incoming = passed.astype(jnp.bfloat16)
            else:
                total = total + passed
        input_grads.append(total)
    stacked = jnp.stack(input_grads)
    row_grads = stacked.reshape(MB, BATCH, F, E).transpose(1, 0, 2, 3).reshape(-1, E)
    index = (owners[..., 0].reshape(-1) * ROWS_DEV + row_ids.reshape(-1)).astype(jnp.int32)
    table_grad = jax.ops.segment_sum(row_grads, index, num_segments=ROWS_DEV * N_SECTION * N_DP)
    return grad_down, grad_up, grad_bias, table_grad
```

```python
import functools

import jax
import jax.numpy as jnp
from jax import lax
from jax.experimental import pallas as pl
from jax.experimental.pallas import tpu as pltpu
from jax.sharding import PartitionSpec as P

E = 256
ROWS_DEV = 2048
NT = (((1,), (1,)), ((), ()))
TN = (((0,), (0,)), ((), ()))
LAG = 3


def relay_kernel(
    sections,
    micro_count,
    rows,
    emb,
    sav,
    cot,
    wd,
    wu,
    bias,
    prod_out,
    glat_out,
    lat_out,
    bias_out,
    home_out,
    gbuf,
    gsend,
    dbuf,
    dsend,
    ubuf,
    usend,
    term_ref,
    gs,
    gr,
    ds,
    dr,
    us,
    ur,
):
    s = lax.axis_index("section")
    chunks = sections * micro_count
    top = sections - 1
    barrier = pltpu.get_barrier_semaphore()

    def greet(step):
        pl.semaphore_signal(
            barrier, inc=1, device_id={"section": s + step}, device_id_type=pl.DeviceIdType.MESH
        )

    @pl.when(s > 0)
    def _():
        greet(-1)

    @pl.when(s < top)
    def _():
        greet(1)

    inner = (s > 0) & (s < top)

    @pl.when(inner)
    def _():
        pl.semaphore_wait(barrier, 2)

    @pl.when(jnp.logical_not(inner))
    def _():
        pl.semaphore_wait(barrier, 1)

    def copy(src, dst, send, recv, j, step):
        return pltpu.make_async_remote_copy(
            src_ref=src.at[j],
            dst_ref=dst.at[j],
            send_sem=send.at[j],
            recv_sem=recv.at[j],
            device_id={"section": s + step},
            device_id_type=pl.DeviceIdType.MESH,
        )

    def g_copy(j):
        return copy(gsend, gbuf, gs, gr, j, -1)

    def d_copy(j):
        return copy(dsend, dbuf, ds, dr, j, -1)

    def u_copy(j):
        return copy(usend, ubuf, us, ur, j, 1)

    bias_out[...] = jnp.zeros_like(bias_out)

    def main(j):
        q = top - j // micro_count
        m = j % micro_count
        at = pl.ds(pl.multiple_of(q * rows, rows), rows)

        @pl.when(s == top)
        def _():
            gbuf[j] = cot[m, at, :]

        @pl.when(s < top)
        def _():
            g_copy(j).wait_recv()

        g32 = gbuf[j].astype(jnp.float32)
        gp = g32 * emb[m, at, :].astype(jnp.float32)
        gpb = gp.astype(jnp.bfloat16)
        prod_out[m, at, :] = gpb
        bias_out[...] += jnp.sum(gp, axis=0, keepdims=True)
        glat = lax.dot_general(gpb, wu[...], NT, preferred_element_type=jnp.float32).astype(
            jnp.bfloat16
        )
        glat_out[m, at, :] = glat
        passed = gbuf[j].astype(jnp.float32) + jnp.dot(
            glat, wd[...], preferred_element_type=jnp.float32
        )

        @pl.when(s > 0)
        def _():
            gsend[j] = passed.astype(jnp.bfloat16)
            g_copy(j).start()
            term_ref[j] = jnp.zeros(term_ref.shape[1:], jnp.float32)

        @pl.when(s == 0)
        def _():
            term_ref[j] = passed

        lat = lax.dot_general(
            sav[m, at, :], wd[...], NT, preferred_element_type=jnp.float32
        ).astype(jnp.bfloat16)
        lat_out[m, at, :] = lat
        product = jnp.dot(lat, wu[...], preferred_element_type=jnp.float32) + bias[...]
        term_ref[j] += gbuf[j].astype(jnp.float32) * product

        @pl.when((s >= q) & (s < top))
        def _():
            d_copy(j).wait_recv()
            term_ref[j] += dbuf[j].astype(jnp.float32)

        @pl.when(s > q)
        def _():
            dsend[j] = term_ref[j].astype(jnp.bfloat16)
            d_copy(j).start()

    def upward(j):
        q = top - j // micro_count
        m = j % micro_count

        @pl.when((s > 0) & (s <= q))
        def _():
            u_copy(j).wait_recv()
            term_ref[j] += ubuf[j].astype(jnp.float32)

        @pl.when(s < q)
        def _():
            usend[j] = term_ref[j].astype(jnp.bfloat16)
            u_copy(j).start()

        @pl.when(s == q)
        def _():
            home_out[m] = term_ref[j].astype(jnp.bfloat16)

    def step(i, carry):
        @pl.when(i < chunks)
        def _():
            main(i)

        j = i - LAG * s

        @pl.when((j >= 0) & (j < chunks))
        def _():
            upward(j)

        return carry

    lax.fori_loop(0, chunks + LAG * top, step, 0)

    def finish(j, carry):
        q = top - j // micro_count

        @pl.when(s > 0)
        def _():
            g_copy(j).wait_send()

        @pl.when(s > q)
        def _():
            d_copy(j).wait_send()

        @pl.when(s < q)
        def _():
            u_copy(j).wait_send()

        return carry

    lax.fori_loop(0, chunks, finish, 0)


def relay(sections, embedded, saved, cotangent, down, up, bias):
    micro_count, samples, width = embedded.shape
    rank = down.shape[0]
    rows = samples // sections
    chunks = sections * micro_count
    b16, f32 = jnp.bfloat16, jnp.float32
    vm = pl.BlockSpec(memory_space=pltpu.VMEM)
    dma = pltpu.SemaphoreType.DMA((chunks,))
    block = pltpu.VMEM((chunks, rows, width), b16)
    return pl.pallas_call(
        functools.partial(relay_kernel, sections, micro_count, rows),
        out_shape=(
            jax.ShapeDtypeStruct((micro_count, samples, width), b16),
            jax.ShapeDtypeStruct((micro_count, samples, rank), b16),
            jax.ShapeDtypeStruct((micro_count, samples, rank), b16),
            jax.ShapeDtypeStruct((1, width), f32),
            jax.ShapeDtypeStruct((micro_count, rows, width), b16),
        ),
        in_specs=[vm] * 6,
        out_specs=(vm,) * 5,
        scratch_shapes=[block] * 6 + [pltpu.VMEM((chunks, rows, width), f32)] + [dma] * 6,
        compiler_params=pltpu.CompilerParams(
            collective_id=0, has_side_effects=True, vmem_limit_bytes=56 * 1024 * 1024
        ),
        cost_estimate=pl.CostEstimate(
            flops=8 * micro_count * samples * width * rank,
            bytes_accessed=300_000_000,
            transcendentals=0,
        ),
    )(embedded, saved, cotangent, down, up, bias)


def local(embedded, saved_inputs, cotangent, w_down, w_up, bias, owners, row_ids):
    sections = lax.axis_size("section")
    replicas = lax.axis_size("dp")
    section_id = lax.axis_index("section")
    micro_count, samples, width = embedded.shape
    b16, f32 = jnp.bfloat16, jnp.float32
    devices = sections * replicas
    sub_rows = samples // sections
    features = width // E

    def home(array):
        array = array.reshape(samples, micro_count, features)
        part = lax.dynamic_slice_in_dim(array, section_id * sub_rows, sub_rows, 0)
        return part.transpose(1, 0, 2).reshape(-1)

    own = home(owners)
    ids = home(row_ids)
    look = own.shape[0]
    capacity = max(2, (2 * look + devices - 1) // devices)
    targets = own[:, None] == jnp.arange(devices, dtype=jnp.int32)[None, :]
    order = jnp.arange(look, dtype=jnp.int32)
    before = (order[None, :] < order[:, None]).astype(b16)
    ranks = jnp.dot(before, targets.astype(b16), preferred_element_type=f32)
    rank_of = jnp.sum(jnp.where(targets, ranks, 0.0), axis=1).astype(jnp.int32)
    place = own * capacity + rank_of
    slots = jnp.arange(devices * capacity, dtype=jnp.int32)
    pick = (slots[:, None] == place[None, :]).astype(b16)
    digits = jnp.stack([ids // 64, ids % 64], axis=1).astype(b16)
    send_digits = jnp.dot(pick, digits, preferred_element_type=f32).astype(jnp.int32)
    send_rows = (send_digits[:, 0] * 64 + send_digits[:, 1]).reshape(devices, capacity)
    got_rows = lax.all_to_all(
        send_rows, ("section", "dp"), split_axis=0, concat_axis=0, tiled=True
    ).reshape(-1)

    prods, glat, lat, bias_part, home_grad = relay(
        sections, embedded, saved_inputs[0], cotangent, w_down[0], w_up[0], bias
    )

    flat = lambda array: array.reshape(-1, array.shape[-1])
    part_down = lax.dot_general(
        flat(glat), flat(saved_inputs[0]), TN, preferred_element_type=f32
    ).astype(b16)
    part_up = lax.dot_general(flat(lat), flat(prods), TN, preferred_element_type=f32).astype(b16)
    part = jnp.concatenate([part_down, part_up], axis=0)
    reduced = lax.psum_scatter(part, "dp", scatter_dimension=1, tiled=True).astype(f32)
    rank = w_down.shape[1]
    grad_down = reduced[None, :rank]
    grad_up = reduced[None, rank:]
    bias_all = lax.all_to_all(
        bias_part.reshape(replicas, -1), "dp", split_axis=0, concat_axis=0, tiled=True
    )
    grad_bias = jnp.sum(bias_all, axis=0)[None]

    row_grads = home_grad.reshape(-1, E)
    send_vals = jnp.dot(pick, row_grads, preferred_element_type=f32).astype(b16)
    got_vals = lax.all_to_all(
        send_vals.reshape(devices, capacity, E),
        ("section", "dp"),
        split_axis=0,
        concat_axis=0,
        tiled=True,
    ).reshape(-1, E)
    named = (jnp.arange(ROWS_DEV, dtype=jnp.int32)[:, None] == got_rows[None, :]).astype(b16)
    table_grad = jnp.dot(named, got_vals, preferred_element_type=f32)
    return (grad_down, grad_up, grad_bias, table_grad)


def solution(mesh):
    placed = (
        P(None, "dp", None),
        P("section", None, "dp", None),
        P(None, "dp", None),
        P("section", None, None),
        P("section", None, None),
        P("section", None),
        P("dp", None, None, None),
        P("dp", None, None),
    )
    return jax.shard_map(
        local,
        mesh=mesh,
        in_specs=placed,
        out_specs=(
            P("section", None, "dp"),
            P("section", None, "dp"),
            P("section", "dp"),
            P(("section", "dp"), None),
        ),
        check_vma=False,
    )
```

```python
import functools

import jax
import jax.numpy as jnp
from jax import lax
from jax.experimental import pallas as pl
from jax.experimental.pallas import tpu as pltpu
from jax.sharding import PartitionSpec as P

E = 256
ROWS_DEV = 2048
NT = (((1,), (1,)), ((), ()))
TN = (((0,), (0,)), ((), ()))
LAG = 3


def relay_kernel(
    sections,
    replicas,
    micro_count,
    rows,
    emb,
    sav,
    cot,
    wd,
    wu,
    bias,
    down_out,
    up_out,
    bias_out,
    home_out,
    prod,
    lg,
    gall,
    lall,
    sall,
    gbuf,
    gsend,
    dbuf,
    dsend,
    ubuf,
    usend,
    term_ref,
    gs,
    gr,
    ds,
    dr,
    us,
    ur,
    xs,
    xr,
    ls,
    lr,
    ss,
    sr,
):
    s = lax.axis_index("section")
    d = lax.axis_index("dp")
    cols = gall.shape[-1]
    rank = wd.shape[0]
    chunks = sections * micro_count
    top = sections - 1
    barrier = pltpu.get_barrier_semaphore()

    def greet(step):
        pl.semaphore_signal(
            barrier, inc=1, device_id={"section": s + step}, device_id_type=pl.DeviceIdType.MESH
        )

    @pl.when(s > 0)
    def _():
        greet(-1)

    @pl.when(s < top)
    def _():
        greet(1)

    def meet(k, carry):
        pl.semaphore_signal(
            barrier,
            inc=1,
            device_id={"dp": (d + k) % replicas},
            device_id_type=pl.DeviceIdType.MESH,
        )
        return carry

    lax.fori_loop(1, replicas, meet, 0)
    inner = (s > 0) & (s < top)

    @pl.when(inner)
    def _():
        pl.semaphore_wait(barrier, replicas + 1)

    @pl.when(jnp.logical_not(inner))
    def _():
        pl.semaphore_wait(barrier, replicas)

    def copy(src, dst, send, recv, j, step):
        return pltpu.make_async_remote_copy(
            src_ref=src.at[j],
            dst_ref=dst.at[j],
            send_sem=send.at[j],
            recv_sem=recv.at[j],
            device_id={"section": s + step},
            device_id_type=pl.DeviceIdType.MESH,
        )

    def g_copy(j):
        return copy(gsend, gbuf, gs, gr, j, -1)

    def d_copy(j):
        return copy(dsend, dbuf, ds, dr, j, -1)

    def u_copy(j):
        return copy(usend, ubuf, us, ur, j, 1)

    def spread(src, dst, send, recv, peer):
        return pltpu.make_async_remote_copy(
            src_ref=src,
            dst_ref=dst,
            send_sem=send,
            recv_sem=recv,
            device_id={"dp": peer},
            device_id_type=pl.DeviceIdType.MESH,
        )

    def columns(who):
        return pl.ds(pl.multiple_of(who * cols, cols), cols)

    def block(who):
        return pl.ds(who * micro_count, micro_count)

    def rows_of(q):
        return pl.ds(pl.multiple_of(q * rows, rows), rows)

    def x_copy(k, q, slot):
        peer = (d + k) % replicas
        return spread(
            prod.at[:, rows_of(q), columns(peer)],
            gall.at[block(slot), rows_of(q), :],
            xs.at[k, q],
            xr.at[k, q],
            peer,
        )

    def l_copy(k, q, slot):
        return spread(
            lg.at[:, rows_of(q), :],
            lall.at[block(slot), rows_of(q), :],
            ls.at[k, q],
            lr.at[k, q],
            (d + k) % replicas,
        )

    def s_copy(k, slot):
        peer = (d + k) % replicas
        return spread(
            sav.at[:, :, columns(peer)], sall.at[block(slot)], ss.at[k], sr.at[k], peer
        )

    def send_saved(k, carry):
        s_copy(k, d).start()
        return carry

    lax.fori_loop(1, replicas, send_saved, 0)

    def main(j):
        q = top - j // micro_count
        m = j % micro_count
        at = pl.ds(pl.multiple_of(q * rows, rows), rows)

        @pl.when(s == top)
        def _():
            gbuf[j] = cot[m, at, :]

        @pl.when(s < top)
        def _():
            g_copy(j).wait_recv()

        g32 = gbuf[j].astype(jnp.float32)
        gp = g32 * emb[m, at, :].astype(jnp.float32)
        gpb = gp.astype(jnp.bfloat16)
        prod[m, at, :] = gpb
        glat = lax.dot_general(gpb, wu[...], NT, preferred_element_type=jnp.float32).astype(
            jnp.bfloat16
        )
        lg[m, at, rank:] = glat
        passed = gbuf[j].astype(jnp.float32) + jnp.dot(
            glat, wd[...], preferred_element_type=jnp.float32
        )

        @pl.when(s > 0)
        def _():
            gsend[j] = passed.astype(jnp.bfloat16)
            g_copy(j).start()
            term_ref[j] = jnp.zeros(term_ref.shape[1:], jnp.float32)

        @pl.when(s == 0)
        def _():
            term_ref[j] = passed

        lat = lax.dot_general(
            sav[m, at, :], wd[...], NT, preferred_element_type=jnp.float32
        ).astype(jnp.bfloat16)
        lg[m, at, :rank] = lat
        product = jnp.dot(lat, wu[...], preferred_element_type=jnp.float32) + bias[...]
        term_ref[j] += gbuf[j].astype(jnp.float32) * product

        @pl.when((s >= q) & (s < top))
        def _():
            d_copy(j).wait_recv()
            term_ref[j] += dbuf[j].astype(jnp.float32)

        @pl.when(s > q)
        def _():
            dsend[j] = term_ref[j].astype(jnp.bfloat16)
            d_copy(j).start()

        @pl.when(m == micro_count - 1)
        def _():
            def send(k, carry):
                x_copy(k, q, d).start()
                l_copy(k, q, d).start()
                return carry

            lax.fori_loop(1, replicas, send, 0)

    def upward(j):
        q = top - j // micro_count
        m = j % micro_count

        @pl.when((s > 0) & (s <= q))
        def _():
            u_copy(j).wait_recv()
            term_ref[j] += ubuf[j].astype(jnp.float32)

        @pl.when(s < q)
        def _():
            usend[j] = term_ref[j].astype(jnp.bfloat16)
            u_copy(j).start()

        @pl.when(s == q)
        def _():
            home_out[m] = term_ref[j].astype(jnp.bfloat16)

    def step(i, carry):
        @pl.when(i < chunks)
        def _():
            main(i)

        j = i - LAG * s

        @pl.when((j >= 0) & (j < chunks))
        def _():
            upward(j)

        return carry

    lax.fori_loop(0, chunks + LAG * top, step, 0)

    def finish(j, carry):
        q = top - j // micro_count

        @pl.when(s > 0)
        def _():
            g_copy(j).wait_send()

        @pl.when(s > q)
        def _():
            d_copy(j).wait_send()

        @pl.when(s < q)
        def _():
            u_copy(j).wait_send()

        return carry

    lax.fori_loop(0, chunks, finish, 0)

    gall[block(d)] = prod[:, :, columns(d)]
    lall[block(d)] = lg[...]
    sall[block(d)] = sav[:, :, columns(d)]

    def arrive(k, carry):
        slot = (d - k + replicas) % replicas
        s_copy(k, slot).wait_recv()
        s_copy(k, d).wait_send()

        def quarter(q, inner_carry):
            x_copy(k, q, slot).wait_recv()
            l_copy(k, q, slot).wait_recv()
            x_copy(k, q, d).wait_send()
            l_copy(k, q, d).wait_send()
            return inner_carry

        return lax.fori_loop(0, sections, quarter, carry)

    lax.fori_loop(1, replicas, arrive, 0)
    total = lall.shape[0] * lall.shape[1]
    products = gall[...].reshape(total, cols)
    bias_out[...] = jnp.sum(products.astype(jnp.float32), axis=0, keepdims=True)
    up_out[...] = lax.dot_general(
        lall[:, :, :rank].reshape(total, rank), products, TN, preferred_element_type=jnp.float32
    )
    down_out[...] = lax.dot_general(
        lall[:, :, rank:].reshape(total, rank),
        sall[...].reshape(total, cols),
        TN,
        preferred_element_type=jnp.float32,
    )


def relay(sections, replicas, embedded, saved, cotangent, down, up, bias):
    micro_count, samples, width = embedded.shape
    rank = down.shape[0]
    rows = samples // sections
    chunks = sections * micro_count
    b16, f32 = jnp.bfloat16, jnp.float32
    vm = pl.BlockSpec(memory_space=pltpu.VMEM)
    dma = pltpu.SemaphoreType.DMA((chunks,))
    block = pltpu.VMEM((chunks, rows, width), b16)
    cols = width // replicas
    held = replicas * micro_count
    quarters = pltpu.SemaphoreType.DMA((replicas, sections))
    return pl.pallas_call(
        functools.partial(relay_kernel, sections, replicas, micro_count, rows),
        out_shape=(
            jax.ShapeDtypeStruct((rank, cols), f32),
            jax.ShapeDtypeStruct((rank, cols), f32),
            jax.ShapeDtypeStruct((1, cols), f32),
            jax.ShapeDtypeStruct((micro_count, rows, width), b16),
        ),
        in_specs=[vm] * 6,
        out_specs=(vm,) * 4,
        scratch_shapes=[
            pltpu.VMEM((micro_count, samples, width), b16),
            pltpu.VMEM((micro_count, samples, 2 * rank), b16),
            pltpu.VMEM((held, samples, cols), b16),
            pltpu.VMEM((held, samples, 2 * rank), b16),
            pltpu.VMEM((held, samples, cols), b16),
        ]
        + [block] * 6
        + [pltpu.VMEM((chunks, rows, width), f32)]
        + [dma] * 6
        + [quarters] * 4
        + [pltpu.SemaphoreType.DMA((replicas,))] * 2,
        compiler_params=pltpu.CompilerParams(
            collective_id=0, has_side_effects=True, vmem_limit_bytes=56 * 1024 * 1024
        ),
        cost_estimate=pl.CostEstimate(
            flops=8 * micro_count * samples * width * rank,
            bytes_accessed=300_000_000,
            transcendentals=0,
        ),
    )(embedded, saved, cotangent, down, up, bias)


def local(embedded, saved_inputs, cotangent, w_down, w_up, bias, owners, row_ids):
    sections = lax.axis_size("section")
    replicas = lax.axis_size("dp")
    section_id = lax.axis_index("section")
    micro_count, samples, width = embedded.shape
    b16, f32 = jnp.bfloat16, jnp.float32
    devices = sections * replicas
    sub_rows = samples // sections
    features = width // E

    def home(array):
        array = array.reshape(samples, micro_count, features)
        part = lax.dynamic_slice_in_dim(array, section_id * sub_rows, sub_rows, 0)
        return part.transpose(1, 0, 2).reshape(-1)

    own = home(owners)
    ids = home(row_ids)
    look = own.shape[0]
    capacity = max(2, (2 * look + devices - 1) // devices)
    targets = own[:, None] == jnp.arange(devices, dtype=jnp.int32)[None, :]
    order = jnp.arange(look, dtype=jnp.int32)
    before = (order[None, :] < order[:, None]).astype(b16)
    ranks = jnp.dot(before, targets.astype(b16), preferred_element_type=f32)
    rank_of = jnp.sum(jnp.where(targets, ranks, 0.0), axis=1).astype(jnp.int32)
    place = own * capacity + rank_of
    slots = jnp.arange(devices * capacity, dtype=jnp.int32)
    pick = (slots[:, None] == place[None, :]).astype(b16)
    digits = jnp.stack([ids // 64, ids % 64], axis=1).astype(b16)
    send_digits = jnp.dot(pick, digits, preferred_element_type=f32).astype(jnp.int32)
    send_rows = (send_digits[:, 0] * 64 + send_digits[:, 1]).reshape(devices, capacity)
    got_rows = lax.all_to_all(
        send_rows, ("section", "dp"), split_axis=0, concat_axis=0, tiled=True
    ).reshape(-1)

    grad_down, grad_up, grad_bias, home_grad = relay(
        sections, replicas, embedded, saved_inputs[0], cotangent, w_down[0], w_up[0], bias
    )

    row_grads = home_grad.reshape(-1, E)
    send_vals = jnp.dot(pick, row_grads, preferred_element_type=f32).astype(b16)
    got_vals = lax.all_to_all(
        send_vals.reshape(devices, capacity, E),
        ("section", "dp"),
        split_axis=0,
        concat_axis=0,
        tiled=True,
    ).reshape(-1, E)
    named = (jnp.arange(ROWS_DEV, dtype=jnp.int32)[:, None] == got_rows[None, :]).astype(b16)
    table_grad = jnp.dot(named, got_vals, preferred_element_type=f32)
    return (grad_down[None], grad_up[None], grad_bias, table_grad)


def solution(mesh):
    placed = (
        P(None, "dp", None),
        P("section", None, "dp", None),
        P(None, "dp", None),
        P("section", None, None),
        P("section", None, None),
        P("section", None),
        P("dp", None, None, None),
        P("dp", None, None),
    )
    return jax.shard_map(
        local,
        mesh=mesh,
        in_specs=placed,
        out_specs=(
            P("section", None, "dp"),
            P("section", None, "dp"),
            P("section", "dp"),
            P(("section", "dp"), None),
        ),
        check_vma=False,
    )
```

```python
import functools

import jax
import jax.numpy as jnp
from jax import lax
from jax.experimental import pallas as pl
from jax.experimental.pallas import tpu as pltpu
from jax.sharding import PartitionSpec as P

E = 256
ROWS_DEV = 2048
NT = (((1,), (1,)), ((), ()))
TN = (((0,), (0,)), ((), ()))
LAG = 3
DOWN_LAG = 3


def relay_kernel(
    sections,
    replicas,
    micro_count,
    rows,
    emb,
    sav,
    cot,
    wd,
    wu,
    bias,
    down_out,
    up_out,
    bias_out,
    home_out,
    prod,
    lg,
    gall,
    lall,
    sall,
    gbuf,
    gsend,
    dbuf,
    dsend,
    ubuf,
    usend,
    term_ref,
    gs,
    gr,
    ds,
    dr,
    us,
    ur,
    xs,
    xr,
    ls,
    lr,
    ss,
    sr,
):
    s = lax.axis_index("section")
    d = lax.axis_index("dp")
    cols = gall.shape[-1]
    rank = wd.shape[0]
    chunks = sections * micro_count
    top = sections - 1
    barrier = pltpu.get_barrier_semaphore()

    def greet(step):
        pl.semaphore_signal(
            barrier, inc=1, device_id={"section": s + step}, device_id_type=pl.DeviceIdType.MESH
        )

    @pl.when(s > 0)
    def _():
        greet(-1)

    @pl.when(s < top)
    def _():
        greet(1)

    def meet(k, carry):
        pl.semaphore_signal(
            barrier,
            inc=1,
            device_id={"dp": (d + k) % replicas},
            device_id_type=pl.DeviceIdType.MESH,
        )
        return carry

    lax.fori_loop(1, replicas, meet, 0)
    inner = (s > 0) & (s < top)

    @pl.when(inner)
    def _():
        pl.semaphore_wait(barrier, replicas + 1)

    @pl.when(jnp.logical_not(inner))
    def _():
        pl.semaphore_wait(barrier, replicas)

    def copy(src, dst, send, recv, j, step):
        return pltpu.make_async_remote_copy(
            src_ref=src.at[j],
            dst_ref=dst.at[j],
            send_sem=send.at[j],
            recv_sem=recv.at[j],
            device_id={"section": s + step},
            device_id_type=pl.DeviceIdType.MESH,
        )

    def g_copy(j):
        return copy(gsend, gbuf, gs, gr, j, -1)

    def d_copy(j):
        return copy(dsend, dbuf, ds, dr, j, -1)

    def u_copy(j):
        return copy(usend, ubuf, us, ur, j, 1)

    def spread(src, dst, send, recv, peer):
        return pltpu.make_async_remote_copy(
            src_ref=src,
            dst_ref=dst,
            send_sem=send,
            recv_sem=recv,
            device_id={"dp": peer},
            device_id_type=pl.DeviceIdType.MESH,
        )

    def columns(who):
        return pl.ds(pl.multiple_of(who * cols, cols), cols)

    def block(who):
        return pl.ds(who * micro_count, micro_count)

    def rows_of(q):
        return pl.ds(pl.multiple_of(q * rows, rows), rows)

    def x_copy(k, q, slot):
        peer = (d + k) % replicas
        return spread(
            prod.at[:, rows_of(q), columns(peer)],
            gall.at[block(slot), rows_of(q), :],
            xs.at[k, q],
            xr.at[k, q],
            peer,
        )

    def l_copy(k, q, slot):
        return spread(
            lg.at[:, rows_of(q), :],
            lall.at[block(slot), rows_of(q), :],
            ls.at[k, q],
            lr.at[k, q],
            (d + k) % replicas,
        )

    def s_copy(k, slot):
        peer = (d + k) % replicas
        return spread(
            sav.at[:, :, columns(peer)], sall.at[block(slot)], ss.at[k], sr.at[k], peer
        )

    def send_saved(k, carry):
        s_copy(k, d).start()
        return carry

    lax.fori_loop(1, replicas, send_saved, 0)

    def main(j):
        q = top - j // micro_count
        m = j % micro_count
        at = pl.ds(pl.multiple_of(q * rows, rows), rows)

        @pl.when(s == top)
        def _():
            gbuf[j] = cot[m, at, :]

        @pl.when(s < top)
        def _():
            g_copy(j).wait_recv()

        g32 = gbuf[j].astype(jnp.float32)
        gp = g32 * emb[m, at, :].astype(jnp.float32)
        gpb = gp.astype(jnp.bfloat16)
        prod[m, at, :] = gpb
        glat = lax.dot_general(gpb, wu[...], NT, preferred_element_type=jnp.float32).astype(
            jnp.bfloat16
        )
        lg[m, at, rank:] = glat
        passed = gbuf[j].astype(jnp.float32) + jnp.dot(
            glat, wd[...], preferred_element_type=jnp.float32
        )

        @pl.when(s > 0)
        def _():
            gsend[j] = passed.astype(jnp.bfloat16)
            g_copy(j).start()
            term_ref[j] = jnp.zeros(term_ref.shape[1:], jnp.float32)

        @pl.when(s == 0)
        def _():
            term_ref[j] = passed

        lat = lax.dot_general(
            sav[m, at, :], wd[...], NT, preferred_element_type=jnp.float32
        ).astype(jnp.bfloat16)
        lg[m, at, :rank] = lat
        product = jnp.dot(lat, wu[...], preferred_element_type=jnp.float32) + bias[...]
        term_ref[j] += gbuf[j].astype(jnp.float32) * product

        @pl.when(m == micro_count - 1)
        def _():
            def send(k, carry):
                x_copy(k, q, d).start()
                l_copy(k, q, d).start()
                return carry

            lax.fori_loop(1, replicas, send, 0)

    def downward(j):
        q = top - j // micro_count

        @pl.when((s >= q) & (s < top))
        def _():
            d_copy(j).wait_recv()
            term_ref[j] += dbuf[j].astype(jnp.float32)

        @pl.when(s > q)
        def _():
            dsend[j] = term_ref[j].astype(jnp.bfloat16)
            d_copy(j).start()

    def upward(j):
        q = top - j // micro_count

        @pl.when((s > 0) & (s <= q))
        def _():
            u_copy(j).wait_recv()
            term_ref[j] += ubuf[j].astype(jnp.float32)

        @pl.when(s < q)
        def _():
            usend[j] = term_ref[j].astype(jnp.bfloat16)
            u_copy(j).start()

    def step(i, carry):
        @pl.when(i < chunks)
        def _():
            main(i)

        behind = i - DOWN_LAG

        @pl.when((behind >= 0) & (behind < chunks))
        def _():
            downward(behind)

        j = i - LAG * s

        @pl.when((j >= 0) & (j < chunks))
        def _():
            upward(j)

        return carry

    lax.fori_loop(0, chunks + max(LAG * top, DOWN_LAG), step, 0)
    for m in range(micro_count):
        home_out[m] = term_ref[(top - s) * micro_count + m].astype(jnp.bfloat16)

    def finish(j, carry):
        q = top - j // micro_count

        @pl.when(s > 0)
        def _():
            g_copy(j).wait_send()

        @pl.when(s > q)
        def _():
            d_copy(j).wait_send()

        @pl.when(s < q)
        def _():
            u_copy(j).wait_send()

        return carry

    lax.fori_loop(0, chunks, finish, 0)

    gall[block(d)] = prod[:, :, columns(d)]
    lall[block(d)] = lg[...]
    sall[block(d)] = sav[:, :, columns(d)]

    def arrive(k, carry):
        slot = (d - k + replicas) % replicas
        s_copy(k, slot).wait_recv()
        s_copy(k, d).wait_send()

        def quarter(q, inner_carry):
            x_copy(k, q, slot).wait_recv()
            l_copy(k, q, slot).wait_recv()
            x_copy(k, q, d).wait_send()
            l_copy(k, q, d).wait_send()
            return inner_carry

        return lax.fori_loop(0, sections, quarter, carry)

    lax.fori_loop(1, replicas, arrive, 0)
    total = lall.shape[0] * lall.shape[1]
    products = gall[...].reshape(total, cols)
    bias_out[...] = jnp.sum(products.astype(jnp.float32), axis=0, keepdims=True)
    up_out[...] = lax.dot_general(
        lall[:, :, :rank].reshape(total, rank), products, TN, preferred_element_type=jnp.float32
    )
    down_out[...] = lax.dot_general(
        lall[:, :, rank:].reshape(total, rank),
        sall[...].reshape(total, cols),
        TN,
        preferred_element_type=jnp.float32,
    )


def relay(sections, replicas, embedded, saved, cotangent, down, up, bias):
    micro_count, samples, width = embedded.shape
    rank = down.shape[0]
    rows = samples // sections
    chunks = sections * micro_count
    b16, f32 = jnp.bfloat16, jnp.float32
    vm = pl.BlockSpec(memory_space=pltpu.VMEM)
    dma = pltpu.SemaphoreType.DMA((chunks,))
    block = pltpu.VMEM((chunks, rows, width), b16)
    cols = width // replicas
    held = replicas * micro_count
    quarters = pltpu.SemaphoreType.DMA((replicas, sections))
    return pl.pallas_call(
        functools.partial(relay_kernel, sections, replicas, micro_count, rows),
        out_shape=(
            jax.ShapeDtypeStruct((rank, cols), f32),
            jax.ShapeDtypeStruct((rank, cols), f32),
            jax.ShapeDtypeStruct((1, cols), f32),
            jax.ShapeDtypeStruct((micro_count, rows, width), b16),
        ),
        in_specs=[vm] * 6,
        out_specs=(vm,) * 4,
        scratch_shapes=[
            pltpu.VMEM((micro_count, samples, width), b16),
            pltpu.VMEM((micro_count, samples, 2 * rank), b16),
            pltpu.VMEM((held, samples, cols), b16),
            pltpu.VMEM((held, samples, 2 * rank), b16),
            pltpu.VMEM((held, samples, cols), b16),
        ]
        + [block] * 6
        + [pltpu.VMEM((chunks, rows, width), f32)]
        + [dma] * 6
        + [quarters] * 4
        + [pltpu.SemaphoreType.DMA((replicas,))] * 2,
        compiler_params=pltpu.CompilerParams(
            collective_id=0, has_side_effects=True, vmem_limit_bytes=56 * 1024 * 1024
        ),
        cost_estimate=pl.CostEstimate(
            flops=8 * micro_count * samples * width * rank,
            bytes_accessed=300_000_000,
            transcendentals=0,
        ),
    )(embedded, saved, cotangent, down, up, bias)


def local(embedded, saved_inputs, cotangent, w_down, w_up, bias, owners, row_ids):
    sections = lax.axis_size("section")
    replicas = lax.axis_size("dp")
    section_id = lax.axis_index("section")
    micro_count, samples, width = embedded.shape
    b16, f32 = jnp.bfloat16, jnp.float32
    devices = sections * replicas
    sub_rows = samples // sections
    features = width // E

    def home(array):
        array = array.reshape(samples, micro_count, features)
        part = lax.dynamic_slice_in_dim(array, section_id * sub_rows, sub_rows, 0)
        return part.transpose(1, 0, 2).reshape(-1)

    own = home(owners)
    ids = home(row_ids)
    look = own.shape[0]
    capacity = max(2, (2 * look + devices - 1) // devices)
    targets = own[:, None] == jnp.arange(devices, dtype=jnp.int32)[None, :]
    order = jnp.arange(look, dtype=jnp.int32)
    before = (order[None, :] < order[:, None]).astype(b16)
    ranks = jnp.dot(before, targets.astype(b16), preferred_element_type=f32)
    rank_of = jnp.sum(jnp.where(targets, ranks, 0.0), axis=1).astype(jnp.int32)
    place = own * capacity + rank_of
    slots = jnp.arange(devices * capacity, dtype=jnp.int32)
    pick = (slots[:, None] == place[None, :]).astype(b16)
    digits = jnp.stack([ids // 64, ids % 64], axis=1).astype(b16)
    send_digits = jnp.dot(pick, digits, preferred_element_type=f32).astype(jnp.int32)
    send_rows = (send_digits[:, 0] * 64 + send_digits[:, 1]).reshape(devices, capacity)
    got_rows = lax.all_to_all(
        send_rows, ("section", "dp"), split_axis=0, concat_axis=0, tiled=True
    ).reshape(-1)

    grad_down, grad_up, grad_bias, home_grad = relay(
        sections, replicas, embedded, saved_inputs[0], cotangent, w_down[0], w_up[0], bias
    )

    row_grads = home_grad.reshape(-1, E)
    send_vals = jnp.dot(pick, row_grads, preferred_element_type=f32).astype(b16)
    got_vals = lax.all_to_all(
        send_vals.reshape(devices, capacity, E),
        ("section", "dp"),
        split_axis=0,
        concat_axis=0,
        tiled=True,
    ).reshape(-1, E)
    named = (jnp.arange(ROWS_DEV, dtype=jnp.int32)[:, None] == got_rows[None, :]).astype(b16)
    table_grad = jnp.dot(named, got_vals, preferred_element_type=f32)
    return (grad_down[None], grad_up[None], grad_bias, table_grad)


def solution(mesh):
    placed = (
        P(None, "dp", None),
        P("section", None, "dp", None),
        P(None, "dp", None),
        P("section", None, None),
        P("section", None, None),
        P("section", None),
        P("dp", None, None, None),
        P("dp", None, None),
    )
    return jax.shard_map(
        local,
        mesh=mesh,
        in_specs=placed,
        out_specs=(
            P("section", None, "dp"),
            P("section", None, "dp"),
            P("section", "dp"),
            P(("section", "dp"), None),
        ),
        check_vma=False,
    )
```
